256 devices in a mesh: seq: 32 (over y, z), head: 8 (over x, core).
Axes of the slice: x: 4, y: 4, z: 8, core: 2. Of those that a mesh axis runs over, the one named last changes fastest.
Arguments:
- frames: bfloat16 [98304, 8192], P('seq', 'head'), may hold values from -6 to 6
- state_proj: bfloat16 [256, 98304], P('head', 'seq'), as said below
- log_decay: float32 [128, 98304], P('head', 'seq'), may hold values from -0.7 to 0
- skip_gain: float32 [128], P('head'), may hold values from 0.1 to 1.9
- group_pos: int32 [384], P('seq'), may hold values from 0 to 383, as said below
Outputs:
- mixed: bfloat16 [98304, 8192], P('seq', 'head')
The draws below stay inside these ranges and needn't reach their ends.
Inputs may be any that keep to these rules, and one draw needn't show every extreme that they name: `group_pos`: device d of seq holds in its 12 slots the groups of sequence positions d * 12 to (d + 1) * 12 - 1, each once, in an order drawn from the seed. `state_proj`: entries lie within 5 times their scale, which is the inverse fourth root of 393216.
All inputs are finite; a program needn't handle non-finite values.
Results may differ from the reference program's by a relative error of at most 0.0053.
Values may be sent and summed in bfloat16 or wider, within the bound.
No kernel may reach another device: no remote copies, remote signals or barrier semaphores. Data moves between devices by JAX's collectives and lax.ppermute only.
A program may use at most 128 MiB of HBM per device.

```python
import jax
import jax.numpy as jnp
from jax import lax

HEADS = 128
HEAD_DIM = 64
STATE = 128
GROUP = 256
CH_DEV = 12
GROUPS = 384
SAMPLE_COUNT = 98304


def draw_state_proj(key, part):
    spread = float(STATE * CH_DEV * GROUP) ** (-0.25)
    values = jnp.clip(jax.random.normal(key, (2 * STATE, SAMPLE_COUNT), jnp.float32), -5.0, 5.0)
    return (values * spread).astype(jnp.bfloat16)


def draw_log_decay(key, part):
    lookup_entries = jax.random.split(key, 5)
    pick = jax.random.uniform(lookup_entries[0], (HEADS,), jnp.float32)
    low = jnp.log(0.005 / SAMPLE_COUNT)
    high = jnp.log(0.03)
    rate_head = jnp.exp(low + pick * (high - low))
    reset_keys = jax.random.split(jax.random.fold_in(key, 7001), 6)
    reset_order = jax.random.permutation(reset_keys[0], HEADS)
    reset_head = reset_order < HEADS // 4
    memory_pick = jax.random.uniform(reset_keys[1], (HEADS,), jnp.float32)
    memory_low = jnp.log(0.2 / SAMPLE_COUNT)
    memory_high = jnp.log(2.0 / SAMPLE_COUNT)
    memory_rate = jnp.exp(memory_low + memory_pick * (memory_high - memory_low))
    rate_head = jnp.where(reset_head, memory_rate, rate_head)
    rough = jax.random.uniform(lookup_entries[1], (HEADS, SAMPLE_COUNT), jnp.float32, 0.5, 2.0)
    block_multiplier = jax.random.uniform(lookup_entries[2], (GROUPS,), jnp.float32, 0.5, 2.0)
    block_rows = jnp.repeat(block_multiplier, GROUP)
    natlog_speeds = -rate_head[:, None] * rough * block_rows[None, :]
    packet_span = jax.random.uniform(lookup_entries[3], (SAMPLE_COUNT,), jnp.float32) < 6.0 / SAMPLE_COUNT
    network_level = jax.random.uniform(lookup_entries[4], (HEADS, SAMPLE_COUNT), jnp.float32, 0.22, 0.69)
    shaped = jnp.where(packet_span[None, :], -network_level, natlog_speeds)
    blocks = GROUPS // CH_DEV
    reset_device = jax.random.randint(reset_keys[2], (), blocks // 2, blocks - 1)
    reset_slot = jax.random.randint(reset_keys[3], (), 0, CH_DEV)
    reset_offset = jax.random.randint(reset_keys[4], (), 0, GROUP - 8 + 1)
    reset_start = (reset_device * CH_DEV + reset_slot) * GROUP + reset_offset
    columns = jnp.arange(SAMPLE_COUNT, dtype=jnp.int32)
    reset_cols = (columns >= reset_start) & (columns < reset_start + 8)
    deep_level = jax.random.uniform(reset_keys[5], (HEADS, SAMPLE_COUNT), jnp.float32, 0.6, 0.69)
    deep_mask = reset_head[:, None] & reset_cols[None, :]
    return jnp.where(deep_mask, -deep_level, shaped).astype(jnp.float32)


def draw_group_pos(key, part):
    blocks = GROUPS // CH_DEV
    lookup_entries = jax.random.split(key, blocks)
    orders = jax.vmap(lambda block_key_rows: jax.random.permutation(block_key_rows, CH_DEV))(lookup_entries)
    offsets = jnp.arange(blocks, dtype=jnp.int32)[:, None] * CH_DEV
    return (orders.astype(jnp.int32) + offsets).reshape(-1).astype(jnp.int32)


def shard_levels(own_key, shape, shards, smallest, largest):
    def one(axis_at, parts):
        steps = jax.random.uniform(jax.random.fold_in(jax.random.fold_in(own_key, 6), axis_at), (parts,), jnp.float32, smallest / len(shards), largest / len(shards))
        return jnp.repeat(jnp.exp(steps), shape[axis_at] // parts).reshape((-1,) + (1,) * (len(shape) - axis_at - 1))

    gain = one(*shards[0])
    for cut in shards[1:]:
        gain = gain * one(*cut)
    return gain


def gaussian(own_key, dims, width, limit, cuts=(), kind=jnp.bfloat16):
    entries = jax.random.normal(own_key, dims, jnp.float32) * width
    if len(cuts) > 0:
        entries = shard_levels(own_key, dims, cuts, -0.22, 0.18) * entries
    return jnp.clip(entries, min=-limit, max=limit).astype(kind)


def setup_inputs(seed: int = 0) -> dict:
    splits = jax.random.split(jax.random.key(seed), 6)
    return {
        "frames": gaussian(splits[0], (SAMPLE_COUNT, HEADS * HEAD_DIM), 1.0, 6.0, ((0, 32), (1, 8))),
        "state_proj": draw_state_proj(jax.random.fold_in(splits[5], 71), 0),
        "log_decay": draw_log_decay(jax.random.fold_in(splits[5], 71), 0),
        "skip_gain": jnp.clip(1.0 + 0.18 * jax.random.normal(splits[3], (HEADS,), jnp.float32), 0.1, 1.9),
        "group_pos": draw_group_pos(jax.random.fold_in(splits[5], 71), 0),
    }


def group_terms(inputs, group_in, natlog_speeds):
    running = jnp.cumsum(natlog_speeds, axis=1)
    input_map = group_in[:STATE]
    output_map = group_in[STATE:]
    coupling = jnp.dot(output_map.T, input_map, preferred_element_type=jnp.float32)
    step_ids = jnp.arange(running.shape[1])
    causal = (step_ids[:, None] >= step_ids[None, :])[None]
    log_gap = running[:, :, None] - running[:, None, :]
    decay_table = jnp.where(causal, jnp.exp(jnp.where(causal, log_gap, 0.0)), 0.0)
    weights = lax.optimization_barrier((coupling[None] * decay_table).astype(jnp.bfloat16))
    within = jnp.einsum("hts,shp->thp", weights.astype(jnp.float32), inputs.astype(jnp.float32))
    group_log = running[:, -1]
    carried = lax.optimization_barrier((inputs.astype(jnp.float32) * jnp.exp(group_log[:, None] - running).T[:, :, None]).astype(jnp.bfloat16))
    summary = jnp.einsum("shp,ns->hpn", carried.astype(jnp.float32), input_map.astype(jnp.float32))
    return within, summary, running


def reference(frames, state_proj, log_decay, skip_gain, group_pos):
    group_count = group_pos.shape[0]
    inverse = jnp.zeros((group_count,), jnp.int32).at[group_pos].set(jnp.arange(group_count, dtype=jnp.int32))
    frames_seq = frames.reshape(group_count, GROUP, HEADS, HEAD_DIM)[inverse]
    proj_seq = state_proj.reshape(2 * STATE, group_count, GROUP).transpose(1, 0, 2)[inverse]
    decay_seq = log_decay.reshape(HEADS, group_count, GROUP).transpose(1, 0, 2)[inverse]

    def advance(carry_state, group_item):
        inputs, group_in, natlog_speeds = group_item
        within, summary, running = group_terms(inputs, group_in, natlog_speeds)
        held_state = lax.optimization_barrier(carry_state.astype(jnp.bfloat16))
        output_map = group_in[STATE:]
        across_shards = jnp.einsum("hpn,nt->thp", held_state.astype(jnp.float32), output_map.astype(jnp.float32))
        across_shards = across_shards * jnp.exp(running).T[:, :, None]
        output = (within + across_shards + skip_gain[None, :, None] * inputs.astype(jnp.float32)).astype(jnp.bfloat16)
        carry_state = jnp.exp(running[:, -1])[:, None, None] * carry_state + summary
        return carry_state, output

    empty_state = jnp.zeros((HEADS, HEAD_DIM, STATE), jnp.float32)
    _, outputs = lax.scan(advance, empty_state, (frames_seq, proj_seq, decay_seq))
    return outputs.reshape(group_count * GROUP, HEADS * HEAD_DIM)
```

```python
import functools

import jax
import jax.numpy as jnp
from jax import lax
from jax.experimental import pallas as pl
from jax.experimental.pallas import tpu as pltpu
from jax.sharding import PartitionSpec as P

HEADS = 16
HEAD_DIM = 64
WIDTH = HEADS * HEAD_DIM
STATE = 128
GROUP = 256
CHUNK = 128
SLOTS = 12
CHUNKS = SLOTS * GROUP // CHUNK
FRAMES = SLOTS * GROUP
SHARD = 32
OWNERS = 32
EXTRA = 16
F32, BF16 = jnp.float32, jnp.bfloat16
VMEM_SPEC = pl.BlockSpec(memory_space=pltpu.VMEM)


def split(value, parts):
    out = []
    for _ in range(parts):
        piece = value.astype(BF16)
        out.append(piece)
        value = value - piece.astype(F32)
    return out


def over_heads(value, hot):
    return lax.dot_general(value, hot, (((0,), (0,)), ((), ())), preferred_element_type=F32)


def slot_of(c, pos_ref):
    slot = 0
    for i in range(SLOTS):
        slot = slot + jnp.where(lax.rem(pos_ref[i], SLOTS) == c, i, 0)
    return slot


def block_of_slice(j):
    return slice((j // 8) * 32, (j // 8) * 32 + 32), slice((j % 8) * 128, (j % 8) * 128 + 128)


def summary_kernel(
    pos_ref, place_ref, x_ref, ld_ref, skip_ref, *rest
):
    pieces = rest[:8]
    pay_ref, proj_ref, eg_ref, rows_ref, acc_ref, w_ref, hot_ref, r_ref = rest[8:]
    step = pl.program_id(0)

    @pl.when(step == 0)
    def _():
        head_of_lane = lax.shift_right_logical(lax.broadcasted_iota(jnp.int32, (2 * HEADS, WIDTH), 1), 6)
        row = lax.broadcasted_iota(jnp.int32, (2 * HEADS, WIDTH), 0) & (HEADS - 1)
        hot_ref[...] = jnp.where(head_of_lane == row, 1.0, 0.0).astype(BF16)
        acc_ref[...] = jnp.zeros_like(acc_ref)
        slots = [slot_of(c, pos_ref) for c in range(SLOTS)]
        for i in range(8):
            at = pl.ds(pl.multiple_of(place_ref[i] * SHARD, SHARD), SHARD)
            for c in range(SLOTS):
                lanes = pl.ds(pl.multiple_of(slots[c] * GROUP, GROUP), GROUP)
                proj_ref[at, c * GROUP : (c + 1) * GROUP] = pieces[i][:, lanes]
        for c in range(SLOTS):
            for half in range(2):
                lanes = pl.ds(pl.multiple_of(slots[c] * GROUP + half * CHUNK, CHUNK), CHUNK)
                r_ref[(2 * c + half) * HEADS : (2 * c + half + 1) * HEADS, :] = ld_ref[:, lanes]
        upto = lax.broadcasted_iota(jnp.int32, (CHUNK, CHUNK), 0) <= lax.broadcasted_iota(
            jnp.int32, (CHUNK, CHUNK), 1
        )
        r_ref[...] = jnp.dot(
            r_ref[...], jnp.where(upto, 1.0, 0.0), precision=lax.Precision.HIGHEST, preferred_element_type=F32
        )
        lane = lax.broadcasted_iota(jnp.int32, (HEADS, CHUNK), 1)
        alpha = jnp.zeros((HEADS, CHUNK), F32)
        past = jnp.zeros((HEADS, 1), F32)
        for c in range(CHUNKS):
            r = r_ref[c * HEADS : (c + 1) * HEADS, :]
            pivot = r[:, CHUNK // 2 - 1 : CHUNK // 2]
            alpha = jnp.where(lane == c, pivot + past, alpha)
            past = r[:, CHUNK - 1 :] - pivot
            for k, part in enumerate(split(jnp.exp(pivot - r), 2)):
                eg_ref[c, k * HEADS : (k + 1) * HEADS, :CHUNK] = part
            for k, part in enumerate(split(jnp.exp(r - pivot), 2)):
                eg_ref[c, k * HEADS : (k + 1) * HEADS, CHUNK:] = part
        hot = hot_ref[...]
        rows = over_heads(jnp.concatenate(split(jnp.exp(alpha), 2)), hot)
        rows_ref[:CHUNKS, :] = rows[:CHUNKS, :]
        skip = sum(
            jnp.dot(jnp.broadcast_to(part.astype(F32), (8, HEADS)).astype(BF16), hot[:HEADS], preferred_element_type=F32)
            for part in split(skip_ref[...], 3)
        )
        rows_ref[CHUNKS:, :] = skip
        after = jnp.zeros((HEADS, 1), F32)
        for c in reversed(range(CHUNKS)):
            r = r_ref[c * HEADS : (c + 1) * HEADS, :]
            last = r[:, CHUNK - 1 :]
            for k, part in enumerate(split(jnp.exp((last - r) + after), 2)):
                w_ref[c // 2, k * HEADS : (k + 1) * HEADS, (c % 2) * CHUNK : (c % 2 + 1) * CHUNK] = part
            after = after + last
        decay = jnp.zeros((HEADS, CHUNK), F32)
        for k, part in enumerate(split(jnp.exp(after), 3)):
            decay = jnp.where(lane == k, part.astype(F32), decay)
        decay = over_heads(decay.astype(BF16), hot[:HEADS])[:EXTRA].astype(BF16)
        for j in range(OWNERS):
            pay_ref[j, 32:, :] = decay[:, block_of_slice(j)[1]]

    weight = over_heads(w_ref[step], hot_ref[...])
    scaled = (x_ref[...].astype(F32) * weight).astype(BF16)
    lanes = pl.ds(pl.multiple_of(step * GROUP, GROUP), GROUP)
    acc_ref[...] += jnp.dot(proj_ref[:STATE, lanes], scaled, preferred_element_type=F32)

    @pl.when(step == SLOTS - 1)
    def _():
        for j in range(OWNERS):
            pay_ref[j, :32, :] = acc_ref[block_of_slice(j)].astype(BF16)


def prefix_kernel(in_ref, out_ref):
    carry = jnp.zeros((32, 128), F32)
    for d in range(OWNERS):
        out_ref[d] = carry.astype(BF16)
        decay = in_ref[d, 32:48, :].astype(F32)
        decay = decay[0:1] + decay[1:2] + decay[2:3]
        carry = decay * carry + in_ref[d, :32, :].astype(F32)


def mix_kernel(pos_ref, x_ref, proj_ref, eg_ref, rows_ref, carry_ref, out_ref, held_ref, hot_ref, lhs_ref, rhs_ref):
    step = pl.program_id(0)

    @pl.when(step == 0)
    def _():
        head_of_lane = lax.shift_right_logical(lax.broadcasted_iota(jnp.int32, (2 * HEADS, WIDTH), 1), 6)
        row = lax.broadcasted_iota(jnp.int32, (2 * HEADS, WIDTH), 0) & (HEADS - 1)
        hot_ref[...] = jnp.where(head_of_lane == row, 1.0, 0.0).astype(BF16)
        lhs_ref[CHUNK:, STATE:] = jnp.zeros((STATE, STATE), BF16)
        for j in range(OWNERS):
            held_ref[block_of_slice(j)] = carry_ref[j].astype(F32)

    causal = lax.broadcasted_iota(jnp.int32, (CHUNK, CHUNK), 0) >= lax.broadcasted_iota(
        jnp.int32, (CHUNK, CHUNK), 1
    )
    skip = rows_ref[CHUNKS : CHUNKS + 1, :]
    for half in range(2):
        frames = slice(half * CHUNK, (half + 1) * CHUNK)
        b = proj_ref[:STATE, frames]
        c_t = proj_ref[STATE:, frames].T
        coupling = jnp.dot(c_t, b, preferred_element_type=F32)
        lhs_ref[:CHUNK, :CHUNK] = jnp.where(causal, coupling, 0.0).astype(BF16)
        lhs_ref[:CHUNK, CHUNK:] = c_t
        lhs_ref[CHUNK:, :CHUNK] = b
        held = held_ref[...] * rows_ref[pl.ds(2 * step + half, 1), :]
        scale = over_heads(eg_ref[half], hot_ref[...])
        x = x_ref[frames, :].astype(F32)
        rhs_ref[:CHUNK, :] = (x * scale[:CHUNK]).astype(BF16)
        rhs_ref[CHUNK:, :] = held.astype(BF16)
        both = jnp.dot(lhs_ref[...], rhs_ref[...], preferred_element_type=F32)
        out_ref[frames, :] = (both[:CHUNK] * scale[CHUNK:] + skip * x).astype(BF16)
        held_ref[...] = held + both[CHUNK:]


def shards(frames, state_proj, log_decay, skip_gain, group_pos):
    def permuted(value, steps):
        return lax.ppermute(value, "head", [(i, (i + steps) % 8) for i in range(8)])

    def partner(value):
        return lax.ppermute(value, "head", [(i, i ^ 1) for i in range(8)])

    near = [state_proj] + [permuted(state_proj, 2 * k) for k in (1, 3, 2)]
    pieces = near + [partner(piece) for piece in near]
    me = lax.axis_index("head")
    hops = jnp.array([0, 2, 6, 4], jnp.int32)
    from_ = lax.rem(me + 8 - hops, 8)
    place = jnp.concatenate([from_, from_ ^ 1])

    def x_index(c, pos_ref, *_):
        return (slot_of(c, pos_ref), 0)

    pay, proj, eg, rows = pl.pallas_call(
        summary_kernel,
        grid_spec=pltpu.PrefetchScalarGridSpec(
            num_scalar_prefetch=2,
            grid=(SLOTS,),
            in_specs=[pl.BlockSpec((GROUP, WIDTH), x_index)] + [VMEM_SPEC] * 10,
            out_specs=[VMEM_SPEC] * 4,
            scratch_shapes=[
                pltpu.VMEM((STATE, WIDTH), F32),
                pltpu.VMEM((SLOTS, 2 * HEADS, GROUP), BF16),
                pltpu.VMEM((2 * HEADS, WIDTH), BF16),
                pltpu.VMEM((CHUNKS * HEADS, CHUNK), F32),
            ],
        ),
        out_shape=[
            jax.ShapeDtypeStruct((OWNERS, 32 + EXTRA, 128), BF16),
            jax.ShapeDtypeStruct((2 * STATE, FRAMES), BF16),
            jax.ShapeDtypeStruct((CHUNKS, 2 * HEADS, GROUP), BF16),
            jax.ShapeDtypeStruct((CHUNKS + 8, WIDTH), F32),
        ],
        name="summary",
    )(group_pos, place, frames, log_decay, skip_gain.reshape(1, HEADS), *pieces)
    pay = lax.all_to_all(pay, "seq", 0, 0, tiled=True)
    carry = pl.pallas_call(
        prefix_kernel,
        in_specs=[VMEM_SPEC],
        out_specs=VMEM_SPEC,
        out_shape=jax.ShapeDtypeStruct((OWNERS, 32, 128), BF16),
        name="prefix",
    )(pay)
    carry = lax.all_to_all(carry, "seq", 0, 0, tiled=True)
    return pl.pallas_call(
        mix_kernel,
        grid_spec=pltpu.PrefetchScalarGridSpec(
            num_scalar_prefetch=1,
            grid=(SLOTS,),
            in_specs=[
                pl.BlockSpec((GROUP, WIDTH), x_index),
                pl.BlockSpec((2 * STATE, GROUP), lambda c, *_: (0, c)),
                pl.BlockSpec((2, 2 * HEADS, GROUP), lambda c, *_: (c, 0, 0)),
                VMEM_SPEC,
                VMEM_SPEC,
            ],
            out_specs=pl.BlockSpec((GROUP, WIDTH), lambda c, *_: (c, 0)),
            scratch_shapes=[
                pltpu.VMEM((STATE, WIDTH), F32),
                pltpu.VMEM((2 * HEADS, WIDTH), BF16),
                pltpu.VMEM((CHUNK + STATE, CHUNK + STATE), BF16),
                pltpu.VMEM((CHUNK + STATE, WIDTH), BF16),
            ],
        ),
        out_shape=jax.ShapeDtypeStruct((FRAMES, WIDTH), BF16),
        name="mix",
    )(group_pos, frames, proj, eg, rows, carry)


def solution(mesh):
    return jax.shard_map(
        shards,
        mesh=mesh,
        in_specs=(P("seq", "head"), P("head", "seq"), P("head", "seq"), P("head"), P("seq")),
        out_specs=P("seq", "head"),
        check_vma=False,
    )
```

```python
import functools

import jax
import jax.numpy as jnp
from jax import lax
from jax.experimental import pallas as pl
from jax.experimental.pallas import tpu as pltpu
from jax.sharding import PartitionSpec as P

HEADS = 16
HEAD_DIM = 64
WIDTH = HEADS * HEAD_DIM
STATE = 128
GROUP = 256
CHUNK = 128
SLOTS = 12
CHUNKS = SLOTS * GROUP // CHUNK
FRAMES = SLOTS * GROUP
COLS = CHUNKS * HEADS
SHARD = 32
OWNERS = 32
EXTRA = 8
DECAY_VMEM = 58
WIDE_VMEM = 58
MID_VMEM = 58
WIDE = 256
SPANS = 4
SPAN = FRAMES // SPANS
F32, BF16 = jnp.float32, jnp.bfloat16
VMEM_SPEC = pl.BlockSpec(memory_space=pltpu.VMEM)


def iota(shape, axis):
    return lax.broadcasted_iota(jnp.int32, shape, axis)


def exact_dot(a, b, dims=(((1,), (0,)), ((), ()))):
    return lax.dot_general(a, b, dims, precision=lax.Precision.HIGHEST, preferred_element_type=F32)


def split(value, parts):
    out = []
    for _ in range(parts):
        piece = value.astype(BF16)
        out.append(piece)
        value = value - piece.astype(F32)
    return out


def over_lanes(source, chunk, start, width):
    rows = source.shape[0]
    base = lax.rem(chunk, 8) * HEADS
    head = lax.shift_right_logical(iota((rows, 128), 1), 6)
    return jnp.concatenate(
        [jnp.take_along_axis(source, head + (base + at // HEAD_DIM), axis=1) for at in range(start, start + width, 128)],
        axis=1,
    )


def column_of(chunk):
    return pl.ds(pl.multiple_of((chunk // 8) * 128, 128), 128)


def block_of_slice(j):
    return slice((j // 8) * 32, (j // 8) * 32 + 32), slice((j % 8) * 128, (j % 8) * 128 + 128)


def tile_of(chunk):
    return pl.ds(pl.multiple_of((chunk // 8) * 256, 256), 256)


def heads_of(hot_ref, chunk):
    rows = hot_ref[pl.ds(pl.multiple_of(112 - lax.rem(chunk, 8) * HEADS, HEADS), 128), :]
    return jnp.concatenate([rows, rows], axis=0)


def fill_hot(hot_ref):
    head = iota((256, WIDTH), 0) - 112
    hot_ref[...] = jnp.where(head == lax.shift_right_logical(iota((256, WIDTH), 1), 6), 1.0, 0.0).astype(BF16)


def store_pair(ref, value):
    for k, part in enumerate(split(value, 2)):
        for block in range(COLS // 128):
            ref[:, block * 256 + k * 128 : block * 256 + (k + 1) * 128] = part[:, block * 128 : (block + 1) * 128]


def decay_kernel(
    pos_ref, x_ref, ld_ref, skip_ref,
    slot_ref, scaled_ref, in_ref, out_ref, far_ref, far_pair_ref, total_ref,
    hot_ref, log_ref, w_ref, w_pair_ref, x_all, scaled_all, sems, out_sems,
):
    def fetch(i):
        return pltpu.make_async_copy(x_ref.at[pl.ds(i * GROUP, GROUP), :], x_all.at[i], sems.at[i])

    def put(i):
        return pltpu.make_async_copy(scaled_all.at[i], scaled_ref.at[pl.ds(i * GROUP, GROUP), :], out_sems.at[i])

    for i in range(SLOTS):
        fetch(i).start()
    base = pos_ref[0] - lax.rem(pos_ref[0], SLOTS)
    for i in range(SLOTS):
        place = pos_ref[i] - base
        slot_ref[place] = i
        for half in range(2):
            at = pl.ds(pl.multiple_of((2 * place + half) * HEADS, HEADS), HEADS)
            log_ref[at, :] = ld_ref[:, i * GROUP + half * CHUNK : i * GROUP + (half + 1) * CHUNK]
    upto = iota((CHUNK, CHUNK), 1) <= iota((CHUNK, CHUNK), 0)
    upto = jnp.where(upto, 1.0, 0.0).astype(BF16)
    r = sum(
        lax.dot_general(upto, part, (((1,), (1,)), ((), ())), preferred_element_type=F32)
        for part in split(log_ref[...], 3)
    )
    pivot = r[CHUNK // 2 - 1 : CHUNK // 2, :]
    last = r[CHUNK - 1 :, :]
    row, col = iota((COLS, COLS), 0), iota((COLS, COLS), 1)
    same = ((row ^ col) & (HEADS - 1)) == 0
    later = jnp.where(same & (row > col), 1.0, 0.0).astype(BF16)
    earlier = jnp.where(same & (row < col), 1.0, 0.0).astype(BF16)
    parts = [jnp.broadcast_to(part.astype(F32), (8, COLS)).astype(BF16) for part in split(last, 3)]
    after = sum(jnp.dot(part, later, preferred_element_type=F32) for part in parts)
    prior = sum(jnp.dot(part, earlier, preferred_element_type=F32) for part in parts)
    step_back = pltpu.roll(jnp.broadcast_to(last - pivot, (8, COLS)), HEADS, 1)
    alpha = jnp.where(iota((8, COLS), 1) < HEADS, 0.0, step_back) + pivot
    same = iota((HEADS, COLS), 0) == (iota((HEADS, COLS), 1) & (HEADS - 1))
    skip = exact_dot(jnp.broadcast_to(skip_ref[...], (8, HEADS)), jnp.where(same, 1.0, 0.0))
    weight = jnp.exp((last - r) + after[:1])
    w_ref[...] = weight
    store_pair(w_pair_ref, weight)
    in_ref[:CHUNK, :] = jnp.exp(pivot - r)
    in_ref[CHUNK:, :] = jnp.where(iota((8, COLS), 0) == 0, jnp.exp(alpha), skip)
    store_pair(out_ref, jnp.exp(r - pivot))
    far = jnp.exp(r + prior[:1])
    far_ref[...] = far
    store_pair(far_pair_ref, far)
    total = over_lanes(jnp.exp(after + last)[:, :128], 0, 0, WIDTH)
    hi, mid, low = (part.astype(F32) for part in split(total, 3))
    row = iota((8, WIDTH), 0)
    total_ref[...] = jnp.where(row == 0, hi, jnp.where(row == 1, mid, jnp.where(row == 2, low, 0.0))).astype(BF16)
    fill_hot(hot_ref)

    def scale_slot(i, _):
        fetch(i).wait()
        for half in range(2):
            chunk = 2 * (pos_ref[i] - base) + half
            frames = slice(half * CHUNK, (half + 1) * CHUNK)
            source, pair = w_ref[:, column_of(chunk)], w_pair_ref[:, tile_of(chunk)]
            hot = heads_of(hot_ref, chunk)
            for at in range(0, WIDTH, WIDE):
                lanes = slice(at, at + WIDE)
                if at < WIDTH // 2:
                    weight = jnp.dot(pair, hot[:, lanes], preferred_element_type=F32)
                else:
                    weight = over_lanes(source, chunk, at, WIDE)
                scaled_all[i, frames, lanes] = (x_all[i, frames, lanes].astype(F32) * weight).astype(BF16)
        put(i).start()
        return 0

    lax.fori_loop(0, SLOTS, scale_slot, 0)
    for i in range(SLOTS):
        put(i).wait()


def summary_kernel(scaled_ref, total_ref, *rest):
    pieces, (pay_ref, out_ref, proj_ref, scaled_all, acc_ref, sem, sems, piece_sems) = rest[:8], rest[8:]

    def fetch(k):
        rows = pl.ds(k * SPAN, SPAN)
        return pltpu.make_async_copy(scaled_ref.at[rows, :], scaled_all.at[rows, :], sems.at[k])

    me = lax.axis_index("head")
    loads = []
    for i, hop in enumerate((0, 2, 6, 4)):
        source = lax.rem(me + 8 - hop, 8)
        for j, shard in ((i, source), (i + 4, source ^ 1)):
            rows = pl.ds(pl.multiple_of(shard * SHARD, SHARD), SHARD)
            loads.append(pltpu.make_async_copy(pieces[j], proj_ref.at[rows, :], piece_sems.at[j]))
            loads[-1].start()
    for k in range(SPANS):
        fetch(k).start()
    for load in loads:
        load.wait()
    keep = pltpu.make_async_copy(proj_ref, out_ref, sem)
    keep.start()
    for k in range(SPANS):
        fetch(k).wait()
        rows = slice(k * SPAN, (k + 1) * SPAN)
        for at in range(0, WIDTH, WIDE):
            lanes = slice(at, at + WIDE)
            state = jnp.dot(proj_ref[:STATE, rows], scaled_all[rows, lanes], preferred_element_type=F32)
            if k > 0:
                state = acc_ref[:, lanes] + state
            if k < SPANS - 1:
                acc_ref[:, lanes] = state
                continue
            state = state.astype(BF16)
            for j in range(OWNERS):
                block, wide = block_of_slice(j)
                if at <= wide.start < at + WIDE:
                    pay_ref[j, :32, :] = state[block, wide.start - at : wide.stop - at]
                    pay_ref[j, 32:, :] = total_ref[:, wide]
    keep.wait()


def prefix_kernel(in_ref, out_ref):
    carry = jnp.zeros((32, 128), F32)
    for d in range(OWNERS):
        out_ref[d] = carry.astype(BF16)
        decay = in_ref[d, 32:, :].astype(F32)
        decay = decay[0:1] + decay[1:2] + decay[2:3]
        carry = decay * carry + in_ref[d, :32, :].astype(F32)


def near_kernel(first, slot_ref, x_ref, proj_hbm, in_hbm, scale_hbm, *rest):
    near_ref, ct_ref, last_ref, held_ref, in_ref, out_scale_ref, hot_ref, x_all, proj_all, sems = rest[-10:]
    step = pl.program_id(0)
    half_slots = SLOTS // 2

    def fetch(i):
        start = pl.multiple_of(slot_ref[i + first] * GROUP, GROUP)
        return (
            pltpu.make_async_copy(proj_hbm.at[:, pl.ds(start, GROUP)], proj_all.at[i], sems.at[half_slots + i]),
            pltpu.make_async_copy(x_ref.at[pl.ds(start, GROUP), :], x_all.at[i], sems.at[i]),
        )

    tables = [
        pltpu.make_async_copy(in_hbm, in_ref, sems.at[2 * half_slots]),
        pltpu.make_async_copy(scale_hbm, out_scale_ref, sems.at[2 * half_slots + 1]),
    ]
    if first:
        tables.append(pltpu.make_async_copy(rest[0], held_ref, sems.at[2 * half_slots + 2]))

    @pl.when(step == 0)
    def _():
        for i in range(half_slots):
            for copy in fetch(i):
                copy.start()
            if i == 0:
                for copy in tables:
                    copy.start()
        fill_hot(hot_ref)
        if not first:
            held_ref[...] = jnp.zeros_like(held_ref)
        for copy in tables:
            copy.wait()

    for copy in fetch(step):
        copy.wait()
    causal = iota((CHUNK, CHUNK), 0) >= iota((CHUNK, CHUNK), 1)
    for half in range(2):
        chunk = 2 * (step + first) + half
        frames = slice(half * CHUNK, (half + 1) * CHUNK)
        b = proj_all[step, :STATE, frames]
        c_t = proj_all[step, STATE:, frames].T
        ct_ref[frames, :] = c_t
        coupling = jnp.where(causal, jnp.dot(c_t, b, preferred_element_type=F32), 0.0).astype(BF16)
        left = jnp.concatenate([coupling, c_t], axis=1)
        to_pivot, from_pivot = in_ref[:, column_of(chunk)], out_scale_ref[:, tile_of(chunk)]
        hot = heads_of(hot_ref, chunk)
        for at in range(0, WIDTH, WIDE):
            lanes = slice(at, at + WIDE)
            scale = over_lanes(to_pivot, chunk, at, WIDE)
            x = x_all[step, frames, lanes].astype(F32)
            held = held_ref[:, lanes] * scale[CHUNK : CHUNK + 1]
            scaled = (x * scale[:CHUNK]).astype(BF16)
            held_ref[:, lanes] = held + jnp.dot(b, scaled, preferred_element_type=F32)
            right = jnp.concatenate([scaled, held.astype(BF16)], axis=0)
            mixed = jnp.dot(left, right, preferred_element_type=F32)
            back = jnp.dot(from_pivot, hot[:, lanes], preferred_element_type=F32)
            near_ref[frames, lanes] = (mixed * back + scale[CHUNK + 1 : CHUNK + 2] * x).astype(BF16)

    @pl.when(step == half_slots - 1)
    def _():
        last_ref[...] = held_ref[...]


def finish_kernel(
    near_ref, ct_hbm, far_hbm, far_pair_hbm, carry_hbm,
    out_ref, held_ref, near_all, ct_all, far_ref, far_pair_ref, carry_ref, hot_ref, sems,
):
    step = pl.program_id(0)
    steps = SLOTS // 2

    def fetch(i):
        rows = pl.ds(i * 2 * GROUP, 2 * GROUP)
        return (
            pltpu.make_async_copy(ct_hbm.at[rows, :], ct_all.at[i], sems.at[steps + i]),
            pltpu.make_async_copy(near_ref.at[rows, :], near_all.at[i], sems.at[i]),
        )

    tables = [
        pltpu.make_async_copy(source, target, sems.at[2 * steps + i])
        for i, (source, target) in enumerate(
            ((carry_hbm, carry_ref), (far_hbm, far_ref), (far_pair_hbm, far_pair_ref))
        )
    ]

    @pl.when(step == 0)
    def _():
        for copy in tables:
            copy.start()
        for i in range(steps):
            for copy in fetch(i):
                copy.start()
        fill_hot(hot_ref)
        for copy in tables:
            copy.wait()
        for j in range(OWNERS):
            held_ref[block_of_slice(j)] = carry_ref[j]

    for copy in fetch(step):
        copy.wait()
    for part in range(4):
        chunk = 4 * step + part
        frames = slice(part * CHUNK, (part + 1) * CHUNK)
        c_t = ct_all[step, frames, :]
        hot = heads_of(hot_ref, chunk)
        for at in range(0, WIDTH, WIDE):
            lanes = slice(at, at + WIDE)
            across = jnp.dot(c_t, held_ref[:, lanes], preferred_element_type=F32)
            if at < WIDE:
                far = jnp.dot(far_pair_ref[:, tile_of(chunk)], hot[:, lanes], preferred_element_type=F32)
            else:
                far = over_lanes(far_ref[:, column_of(chunk)], chunk, at, WIDE)
            near = near_all[step, frames, lanes].astype(F32)
            out_ref[frames, lanes] = (near + far * across).astype(BF16)


def shards(frames, state_proj, log_decay, skip_gain, group_pos):
    def permuted(value, steps):
        return lax.ppermute(value, "head", [(i, (i + steps) % 8) for i in range(8)])

    def partner(value):
        return lax.ppermute(value, "head", [(i, i ^ 1) for i in range(8)])

    params = pltpu.CompilerParams(vmem_limit_bytes=16 << 20)
    mid_params = pltpu.CompilerParams(vmem_limit_bytes=MID_VMEM << 20)
    wide_params = pltpu.CompilerParams(vmem_limit_bytes=WIDE_VMEM << 20)
    shape = jax.ShapeDtypeStruct
    slots, scaled, to_pivot, from_pivot, far, far_pair, total = pl.pallas_call(
        decay_kernel,
        in_specs=[
            pl.BlockSpec(memory_space=pltpu.SMEM),
            pl.BlockSpec(memory_space=pltpu.HBM),
            VMEM_SPEC,
            VMEM_SPEC,
        ],
        out_specs=[pl.BlockSpec(memory_space=pltpu.SMEM), pl.BlockSpec(memory_space=pltpu.HBM)] + [VMEM_SPEC] * 5,
        scratch_shapes=[
            pltpu.VMEM((256, WIDTH), BF16),
            pltpu.VMEM((COLS, CHUNK), F32),
            pltpu.VMEM((CHUNK, COLS), F32),
            pltpu.VMEM((CHUNK, 2 * COLS), BF16),
            pltpu.VMEM((SLOTS, GROUP, WIDTH), BF16),
            pltpu.VMEM((SLOTS, GROUP, WIDTH), BF16),
            pltpu.SemaphoreType.DMA((SLOTS,)),
            pltpu.SemaphoreType.DMA((SLOTS,)),
        ],
        out_shape=[
            shape((SLOTS,), jnp.int32),
            shape((FRAMES, WIDTH), BF16),
            shape((CHUNK + 8, COLS), F32),
            shape((CHUNK, 2 * COLS), BF16),
            shape((CHUNK, COLS), F32),
            shape((CHUNK, 2 * COLS), BF16),
            shape((EXTRA, WIDTH), BF16),
        ],
        compiler_params=pltpu.CompilerParams(vmem_limit_bytes=DECAY_VMEM << 20),
        cost_estimate=pl.CostEstimate(flops=10**9, bytes_accessed=14 * 10**6, transcendentals=10**6),
        name="decay",
    )(group_pos, frames, log_decay, skip_gain.reshape(1, HEADS))
    near = [state_proj] + [permuted(state_proj, 2 * k) for k in (1, 3, 2)]
    own_partner = partner(state_proj)
    near, total = lax.optimization_barrier((near, total))
    pieces = near + [own_partner] + [partner(piece) for piece in near[1:]]
    pay, proj = pl.pallas_call(
        summary_kernel,
        in_specs=[pl.BlockSpec(memory_space=pltpu.HBM), VMEM_SPEC] + [pl.BlockSpec(memory_space=pl.ANY)] * 8,
        out_specs=[VMEM_SPEC, pl.BlockSpec(memory_space=pltpu.HBM)],
        scratch_shapes=[
            pltpu.VMEM((2 * STATE, FRAMES), BF16),
            pltpu.VMEM((FRAMES, WIDTH), BF16),
            pltpu.VMEM((STATE, WIDTH), F32),
            pltpu.SemaphoreType.DMA,
            pltpu.SemaphoreType.DMA((SPANS,)),
            pltpu.SemaphoreType.DMA((8,)),
        ],
        out_shape=[shape((OWNERS, 32 + EXTRA, 128), BF16), shape((2 * STATE, FRAMES), BF16)],
        compiler_params=mid_params,
        name="summary",
    )(scaled, total, *pieces)
    pay = lax.all_to_all(pay, "seq", 0, 0, tiled=True)

    def near_call(first, *start_and_done):
        done = start_and_done[1:]

        return pl.pallas_call(
            functools.partial(near_kernel, first),
            grid_spec=pltpu.PrefetchScalarGridSpec(
                num_scalar_prefetch=1,
                grid=(SLOTS // 2,),
                in_specs=[pl.BlockSpec(memory_space=pltpu.HBM)] * (5 if first else 4)
                + [pl.BlockSpec(memory_space=pl.ANY)] * len(done),
                out_specs=[
                    pl.BlockSpec((GROUP, WIDTH), lambda c, *_: (c + first, 0)),
                    pl.BlockSpec((GROUP, STATE), lambda c, *_: (c + first, 0)),
                    VMEM_SPEC,
                ],
                scratch_shapes=[
                    pltpu.VMEM((STATE, WIDTH), F32),
                    pltpu.VMEM((CHUNK + 8, COLS), F32),
                    pltpu.VMEM((CHUNK, 2 * COLS), BF16),
                    pltpu.VMEM((256, WIDTH), BF16),
                    pltpu.VMEM((SLOTS // 2, GROUP, WIDTH), BF16),
                    pltpu.VMEM((SLOTS // 2, 2 * STATE, GROUP), BF16),
                    pltpu.SemaphoreType.DMA((SLOTS + 3,)),
                ],
            ),
            out_shape=[shape((FRAMES, WIDTH), BF16), shape((FRAMES, STATE), BF16), shape((STATE, WIDTH), F32)],
            input_output_aliases={6 + i: i for i in range(len(done))},
            compiler_params=wide_params,
            cost_estimate=pl.CostEstimate(flops=3 * 10**9, bytes_accessed=20 * 10**6, transcendentals=0),
            name="near",
        )(slots, frames, proj, to_pivot, from_pivot, *start_and_done)

    near, c_t, held = near_call(0)
    pay, held = lax.optimization_barrier((pay, held))
    carry = pl.pallas_call(
        prefix_kernel,
        in_specs=[VMEM_SPEC],
        out_specs=VMEM_SPEC,
        out_shape=shape((OWNERS, 32, 128), BF16),
        compiler_params=params,
        name="prefix",
    )(pay)
    carry = lax.all_to_all(carry, "seq", 0, 0, tiled=True)
    near, c_t, held = near_call(SLOTS // 2, held, near, c_t)
    return pl.pallas_call(
        finish_kernel,
        grid=(SLOTS // 2,),
        in_specs=[pl.BlockSpec(memory_space=pltpu.HBM)] * 2 + [pl.BlockSpec(memory_space=pl.ANY)] * 3,
        out_specs=pl.BlockSpec((2 * GROUP, WIDTH), lambda c: (c, 0)),
        scratch_shapes=[
            pltpu.VMEM((STATE, WIDTH), BF16),
            pltpu.VMEM((SLOTS // 2, 2 * GROUP, WIDTH), BF16),
            pltpu.VMEM((SLOTS // 2, 2 * GROUP, STATE), BF16),
            pltpu.VMEM((CHUNK, COLS), F32),
            pltpu.VMEM((CHUNK, 2 * COLS), BF16),
            pltpu.VMEM((OWNERS, 32, 128), BF16),
            pltpu.VMEM((256, WIDTH), BF16),
            pltpu.SemaphoreType.DMA((SLOTS + 3,)),
        ],
        out_shape=shape((FRAMES, WIDTH), BF16),
        compiler_params=mid_params,
        name="finish",
    )(near, c_t, far, far_pair, carry)


def solution(mesh):
    return jax.shard_map(
        shards,
        mesh=mesh,
        in_specs=(P("seq", "head"), P("head", "seq"), P("head", "seq"), P("head"), P("seq")),
        out_specs=P("seq", "head"),
        check_vma=False,
    )
```

```python
import functools

import jax
import jax.numpy as jnp
from jax import lax
from jax.experimental import pallas as pl
from jax.experimental.pallas import tpu as pltpu
from jax.sharding import PartitionSpec as P

HEADS = 16
HEAD_DIM = 64
WIDTH = HEADS * HEAD_DIM
STATE = 128
GROUP = 256
CHUNK = 128
SLOTS = 12
CHUNKS = SLOTS * GROUP // CHUNK
FRAMES = SLOTS * GROUP
COLS = CHUNKS * HEADS
SHARD = 32
OWNERS = 32
EXTRA = 8
DECAY_VMEM = 44
SUMMARY_VMEM = 16
WIDE_VMEM = 58
MID_VMEM = 53
WIDE = 256
F32, BF16 = jnp.float32, jnp.bfloat16
VMEM_SPEC = pl.BlockSpec(memory_space=pltpu.VMEM)


def iota(shape, axis):
    return lax.broadcasted_iota(jnp.int32, shape, axis)


def exact_dot(a, b, dims=(((1,), (0,)), ((), ()))):
    return lax.dot_general(a, b, dims, precision=lax.Precision.HIGHEST, preferred_element_type=F32)


def split(value, parts):
    out = []
    for _ in range(parts):
        piece = value.astype(BF16)
        out.append(piece)
        value = value - piece.astype(F32)
    return out


def over_lanes(source, chunk, start, width):
    rows = source.shape[0]
    base = lax.rem(chunk, 8) * HEADS
    head = lax.shift_right_logical(iota((rows, 128), 1), 6)
    return jnp.concatenate(
        [jnp.take_along_axis(source, head + (base + at // HEAD_DIM), axis=1) for at in range(start, start + width, 128)],
        axis=1,
    )


def column_of(chunk):
    return pl.ds(pl.multiple_of((chunk // 8) * 128, 128), 128)


def block_of_slice(j):
    return slice((j // 8) * 32, (j // 8) * 32 + 32), slice((j % 8) * 128, (j % 8) * 128 + 128)


def tile_of(chunk):
    return pl.ds(pl.multiple_of((chunk // 8) * 256, 256), 256)


def heads_of(hot_ref, chunk):
    rows = hot_ref[pl.ds(pl.multiple_of(112 - lax.rem(chunk, 8) * HEADS, HEADS), 128), :]
    return jnp.concatenate([rows, rows], axis=0)


def fill_hot(hot_ref):
    head = iota((256, WIDTH), 0) - 112
    hot_ref[...] = jnp.where(head == lax.shift_right_logical(iota((256, WIDTH), 1), 6), 1.0, 0.0).astype(BF16)


def store_pair(ref, value):
    for k, part in enumerate(split(value, 2)):
        for block in range(COLS // 128):
            ref[:, block * 256 + k * 128 : block * 256 + (k + 1) * 128] = part[:, block * 128 : (block + 1) * 128]


def decay_kernel(
    pos_ref, x_ref, ld_ref, skip_ref,
    slot_ref, scaled_ref, in_ref, out_ref, far_ref, far_pair_ref, total_ref,
    hot_ref, log_ref, w_ref, w_pair_ref, x_all, sems,
):
    def fetch(i):
        return pltpu.make_async_copy(x_ref.at[pl.ds(i * GROUP, GROUP), :], x_all.at[i], sems.at[i])

    for i in range(SLOTS):
        fetch(i).start()
    base = pos_ref[0] - lax.rem(pos_ref[0], SLOTS)
    for i in range(SLOTS):
        place = pos_ref[i] - base
        slot_ref[place] = i
        for half in range(2):
            at = pl.ds(pl.multiple_of((2 * place + half) * HEADS, HEADS), HEADS)
            log_ref[at, :] = ld_ref[:, i * GROUP + half * CHUNK : i * GROUP + (half + 1) * CHUNK]
    upto = iota((CHUNK, CHUNK), 1) <= iota((CHUNK, CHUNK), 0)
    upto = jnp.where(upto, 1.0, 0.0).astype(BF16)
    r = sum(
        lax.dot_general(upto, part, (((1,), (1,)), ((), ())), preferred_element_type=F32)
        for part in split(log_ref[...], 3)
    )
    pivot = r[CHUNK // 2 - 1 : CHUNK // 2, :]
    last = r[CHUNK - 1 :, :]
    row, col = iota((COLS, COLS), 0), iota((COLS, COLS), 1)
    same = ((row ^ col) & (HEADS - 1)) == 0
    later = jnp.where(same & (row > col), 1.0, 0.0).astype(BF16)
    earlier = jnp.where(same & (row < col), 1.0, 0.0).astype(BF16)
    parts = [jnp.broadcast_to(part.astype(F32), (8, COLS)).astype(BF16) for part in split(last, 3)]
    after = sum(jnp.dot(part, later, preferred_element_type=F32) for part in parts)
    prior = sum(jnp.dot(part, earlier, preferred_element_type=F32) for part in parts)
    step_back = pltpu.roll(jnp.broadcast_to(last - pivot, (8, COLS)), HEADS, 1)
    alpha = jnp.where(iota((8, COLS), 1) < HEADS, 0.0, step_back) + pivot
    same = iota((HEADS, COLS), 0) == (iota((HEADS, COLS), 1) & (HEADS - 1))
    skip = exact_dot(jnp.broadcast_to(skip_ref[...], (8, HEADS)), jnp.where(same, 1.0, 0.0))
    weight = jnp.exp((last - r) + after[:1])
    w_ref[...] = weight
    store_pair(w_pair_ref, weight)
    in_ref[:CHUNK, :] = jnp.exp(pivot - r)
    in_ref[CHUNK:, :] = jnp.where(iota((8, COLS), 0) == 0, jnp.exp(alpha), skip)
    store_pair(out_ref, jnp.exp(r - pivot))
    far = jnp.exp(r + prior[:1])
    far_ref[...] = far
    store_pair(far_pair_ref, far)
    total = over_lanes(jnp.exp(after + last)[:, :128], 0, 0, WIDTH)
    hi, mid, low = (part.astype(F32) for part in split(total, 3))
    row = iota((8, WIDTH), 0)
    total_ref[...] = jnp.where(row == 0, hi, jnp.where(row == 1, mid, jnp.where(row == 2, low, 0.0))).astype(BF16)
    fill_hot(hot_ref)

    def scale_slot(i, _):
        fetch(i).wait()
        for half in range(2):
            chunk = 2 * (pos_ref[i] - base) + half
            frames = slice(half * CHUNK, (half + 1) * CHUNK)
            source, pair = w_ref[:, column_of(chunk)], w_pair_ref[:, tile_of(chunk)]
            hot = heads_of(hot_ref, chunk)
            for at in range(0, WIDTH, WIDE):
                lanes = slice(at, at + WIDE)
                if at < WIDTH // 2:
                    weight = jnp.dot(pair, hot[:, lanes], preferred_element_type=F32)
                else:
                    weight = over_lanes(source, chunk, at, WIDE)
                scaled_ref[pl.ds(pl.multiple_of(i * GROUP + half * CHUNK, CHUNK), CHUNK), lanes] = (x_all[i, frames, lanes].astype(F32) * weight).astype(BF16)
        return 0

    lax.fori_loop(0, SLOTS, scale_slot, 0)


def summary_kernel(scaled_ref, total_ref, *rest):
    pieces, (pay_ref, out_ref, proj_ref, sem) = rest[:8], rest[8:]
    me = lax.axis_index("head")
    for i, hop in enumerate((0, 2, 6, 4)):
        source = lax.rem(me + 8 - hop, 8)
        proj_ref[pl.ds(pl.multiple_of(source * SHARD, SHARD), SHARD), :] = pieces[i][...]
        proj_ref[pl.ds(pl.multiple_of((source ^ 1) * SHARD, SHARD), SHARD), :] = pieces[i + 4][...]
    keep = pltpu.make_async_copy(proj_ref, out_ref, sem)
    keep.start()
    for at in range(0, WIDTH, WIDE):
        state = jnp.dot(proj_ref[:STATE, :], scaled_ref[:, at : at + WIDE], preferred_element_type=F32).astype(BF16)
        for j in range(OWNERS):
            rows, lanes = block_of_slice(j)
            if at <= lanes.start < at + WIDE:
                pay_ref[j, :32, :] = state[rows, lanes.start - at : lanes.stop - at]
                pay_ref[j, 32:, :] = total_ref[:, lanes]
    keep.wait()


def prefix_kernel(in_ref, out_ref):
    carry = jnp.zeros((32, 128), F32)
    for d in range(OWNERS):
        out_ref[d] = carry.astype(BF16)
        decay = in_ref[d, 32:, :].astype(F32)
        decay = decay[0:1] + decay[1:2] + decay[2:3]
        carry = decay * carry + in_ref[d, :32, :].astype(F32)


def near_kernel(first, slot_ref, x_ref, proj_hbm, in_hbm, scale_hbm, *rest):
    near_ref, ct_ref, last_ref, held_ref, in_ref, out_scale_ref, hot_ref, x_all, proj_all, sems = rest[-10:]
    step = pl.program_id(0)
    half_slots = SLOTS // 2

    def fetch(i):
        start = pl.multiple_of(slot_ref[i + first] * GROUP, GROUP)
        return (
            pltpu.make_async_copy(proj_hbm.at[:, pl.ds(start, GROUP)], proj_all.at[i], sems.at[half_slots + i]),
            pltpu.make_async_copy(x_ref.at[pl.ds(start, GROUP), :], x_all.at[i], sems.at[i]),
        )

    tables = [
        pltpu.make_async_copy(in_hbm, in_ref, sems.at[2 * half_slots]),
        pltpu.make_async_copy(scale_hbm, out_scale_ref, sems.at[2 * half_slots + 1]),
    ]
    if first:
        tables.append(pltpu.make_async_copy(rest[0], held_ref, sems.at[2 * half_slots + 2]))

    @pl.when(step == 0)
    def _():
        for i in range(half_slots):
            for copy in fetch(i):
                copy.start()
            if i == 0:
                for copy in tables:
                    copy.start()
        fill_hot(hot_ref)
        if not first:
            held_ref[...] = jnp.zeros_like(held_ref)
        for copy in tables:
            copy.wait()

    for copy in fetch(step):
        copy.wait()
    causal = iota((CHUNK, CHUNK), 0) >= iota((CHUNK, CHUNK), 1)
    for half in range(2):
        chunk = 2 * (step + first) + half
        frames = slice(half * CHUNK, (half + 1) * CHUNK)
        b = proj_all[step, :STATE, frames]
        c_t = proj_all[step, STATE:, frames].T
        ct_ref[frames, :] = c_t
        coupling = jnp.where(causal, jnp.dot(c_t, b, preferred_element_type=F32), 0.0).astype(BF16)
        left = jnp.concatenate([coupling, c_t], axis=1)
        to_pivot, from_pivot = in_ref[:, column_of(chunk)], out_scale_ref[:, tile_of(chunk)]
        hot = heads_of(hot_ref, chunk)
        for at in range(0, WIDTH, WIDE):
            lanes = slice(at, at + WIDE)
            scale = over_lanes(to_pivot, chunk, at, WIDE)
            x = x_all[step, frames, lanes].astype(F32)
            held = held_ref[:, lanes] * scale[CHUNK : CHUNK + 1]
            scaled = (x * scale[:CHUNK]).astype(BF16)
            held_ref[:, lanes] = held + jnp.dot(b, scaled, preferred_element_type=F32)
            right = jnp.concatenate([scaled, held.astype(BF16)], axis=0)
            mixed = jnp.dot(left, right, preferred_element_type=F32)
            back = jnp.dot(from_pivot, hot[:, lanes], preferred_element_type=F32)
            near_ref[frames, lanes] = (mixed * back + scale[CHUNK + 1 : CHUNK + 2] * x).astype(BF16)

    @pl.when(step == half_slots - 1)
    def _():
        last_ref[...] = held_ref[...]


def finish_kernel(
    near_ref, ct_hbm, far_hbm, far_pair_hbm, carry_hbm,
    out_ref, held_ref, near_all, ct_all, far_ref, far_pair_ref, carry_ref, hot_ref, sems,
):
    step = pl.program_id(0)
    steps = SLOTS // 2

    def fetch(i):
        rows = pl.ds(i * 2 * GROUP, 2 * GROUP)
        return (
            pltpu.make_async_copy(ct_hbm.at[rows, :], ct_all.at[i], sems.at[steps + i]),
            pltpu.make_async_copy(near_ref.at[rows, :], near_all.at[i], sems.at[i]),
        )

    tables = [
        pltpu.make_async_copy(source, target, sems.at[2 * steps + i])
        for i, (source, target) in enumerate(
            ((carry_hbm, carry_ref), (far_hbm, far_ref), (far_pair_hbm, far_pair_ref))
        )
    ]

    @pl.when(step == 0)
    def _():
        for copy in tables:
            copy.start()
        for i in range(steps):
            for copy in fetch(i):
                copy.start()
        fill_hot(hot_ref)
        for copy in tables:
            copy.wait()
        for j in range(OWNERS):
            held_ref[block_of_slice(j)] = carry_ref[j]

    for copy in fetch(step):
        copy.wait()
    for part in range(4):
        chunk = 4 * step + part
        frames = slice(part * CHUNK, (part + 1) * CHUNK)
        c_t = ct_all[step, frames, :]
        hot = heads_of(hot_ref, chunk)
        for at in range(0, WIDTH, WIDE):
            lanes = slice(at, at + WIDE)
            across = jnp.dot(c_t, held_ref[:, lanes], preferred_element_type=F32)
            if at < WIDE:
                far = jnp.dot(far_pair_ref[:, tile_of(chunk)], hot[:, lanes], preferred_element_type=F32)
            else:
                far = over_lanes(far_ref[:, column_of(chunk)], chunk, at, WIDE)
            near = near_all[step, frames, lanes].astype(F32)
            out_ref[frames, lanes] = (near + far * across).astype(BF16)


def shards(frames, state_proj, log_decay, skip_gain, group_pos):
    def permuted(value, steps):
        return lax.ppermute(value, "head", [(i, (i + steps) % 8) for i in range(8)])

    def partner(value):
        return lax.ppermute(value, "head", [(i, i ^ 1) for i in range(8)])

    params = pltpu.CompilerParams(vmem_limit_bytes=16 << 20)
    mid_params = pltpu.CompilerParams(vmem_limit_bytes=MID_VMEM << 20)
    wide_params = pltpu.CompilerParams(vmem_limit_bytes=WIDE_VMEM << 20)
    shape = jax.ShapeDtypeStruct
    slots, scaled, to_pivot, from_pivot, far, far_pair, total = pl.pallas_call(
        decay_kernel,
        in_specs=[
            pl.BlockSpec(memory_space=pltpu.SMEM),
            pl.BlockSpec(memory_space=pltpu.HBM),
            VMEM_SPEC,
            VMEM_SPEC,
        ],
        out_specs=[pl.BlockSpec(memory_space=pltpu.SMEM)] + [VMEM_SPEC] * 6,
        scratch_shapes=[
            pltpu.VMEM((256, WIDTH), BF16),
            pltpu.VMEM((COLS, CHUNK), F32),
            pltpu.VMEM((CHUNK, COLS), F32),
            pltpu.VMEM((CHUNK, 2 * COLS), BF16),
            pltpu.VMEM((SLOTS, GROUP, WIDTH), BF16),
            pltpu.SemaphoreType.DMA((SLOTS,)),
        ],
        out_shape=[
            shape((SLOTS,), jnp.int32),
            shape((FRAMES, WIDTH), BF16),
            shape((CHUNK + 8, COLS), F32),
            shape((CHUNK, 2 * COLS), BF16),
            shape((CHUNK, COLS), F32),
            shape((CHUNK, 2 * COLS), BF16),
            shape((EXTRA, WIDTH), BF16),
        ],
        compiler_params=pltpu.CompilerParams(vmem_limit_bytes=DECAY_VMEM << 20),
        cost_estimate=pl.CostEstimate(flops=10**9, bytes_accessed=14 * 10**6, transcendentals=10**6),
        name="decay",
    )(group_pos, frames, log_decay, skip_gain.reshape(1, HEADS))
    near = [state_proj] + [permuted(state_proj, 2 * k) for k in (1, 3, 2)]
    own_partner = partner(state_proj)
    near, total = lax.optimization_barrier((near, total))
    pieces = near + [own_partner] + [partner(piece) for piece in near[1:]]
    pay, proj = pl.pallas_call(
        summary_kernel,
        in_specs=[VMEM_SPEC] * 10,
        out_specs=[VMEM_SPEC, pl.BlockSpec(memory_space=pltpu.HBM)],
        scratch_shapes=[
            pltpu.VMEM((2 * STATE, FRAMES), BF16),
            pltpu.SemaphoreType.DMA,
        ],
        out_shape=[shape((OWNERS, 32 + EXTRA, 128), BF16), shape((2 * STATE, FRAMES), BF16)],
        compiler_params=pltpu.CompilerParams(vmem_limit_bytes=SUMMARY_VMEM << 20),
        name="summary",
    )(scaled, total, *pieces)
    pay = lax.all_to_all(pay, "seq", 0, 0, tiled=True)

    def near_call(first, *start_and_done):
        done = start_and_done[1:]

        return pl.pallas_call(
            functools.partial(near_kernel, first),
            grid_spec=pltpu.PrefetchScalarGridSpec(
                num_scalar_prefetch=1,
                grid=(SLOTS // 2,),
                in_specs=[pl.BlockSpec(memory_space=pltpu.HBM)] * (5 if first else 4)
                + [pl.BlockSpec(memory_space=pl.ANY)] * len(done),
                out_specs=[
                    pl.BlockSpec((GROUP, WIDTH), lambda c, *_: (c + first, 0)),
                    pl.BlockSpec((GROUP, STATE), lambda c, *_: (c + first, 0)),
                    VMEM_SPEC,
                ],
                scratch_shapes=[
                    pltpu.VMEM((STATE, WIDTH), F32),
                    pltpu.VMEM((CHUNK + 8, COLS), F32),
                    pltpu.VMEM((CHUNK, 2 * COLS), BF16),
                    pltpu.VMEM((256, WIDTH), BF16),
                    pltpu.VMEM((SLOTS // 2, GROUP, WIDTH), BF16),
                    pltpu.VMEM((SLOTS // 2, 2 * STATE, GROUP), BF16),
                    pltpu.SemaphoreType.DMA((SLOTS + 3,)),
                ],
            ),
            out_shape=[shape((FRAMES, WIDTH), BF16), shape((FRAMES, STATE), BF16), shape((STATE, WIDTH), F32)],
            input_output_aliases={6 + i: i for i in range(len(done))},
            compiler_params=wide_params,
            cost_estimate=pl.CostEstimate(flops=3 * 10**9, bytes_accessed=20 * 10**6, transcendentals=0),
            name="near",
        )(slots, frames, proj, to_pivot, from_pivot, *start_and_done)

    near, c_t, held = near_call(0)
    pay, held = lax.optimization_barrier((pay, held))
    carry = pl.pallas_call(
        prefix_kernel,
        in_specs=[VMEM_SPEC],
        out_specs=VMEM_SPEC,
        out_shape=shape((OWNERS, 32, 128), BF16),
        compiler_params=params,
        name="prefix",
    )(pay)
    carry = lax.all_to_all(carry, "seq", 0, 0, tiled=True)
    near, c_t, held = near_call(SLOTS // 2, held, near, c_t)
    return pl.pallas_call(
        finish_kernel,
        grid=(SLOTS // 2,),
        in_specs=[pl.BlockSpec(memory_space=pltpu.HBM)] * 2 + [pl.BlockSpec(memory_space=pl.ANY)] * 3,
        out_specs=pl.BlockSpec((2 * GROUP, WIDTH), lambda c: (c, 0)),
        scratch_shapes=[
            pltpu.VMEM((STATE, WIDTH), BF16),
            pltpu.VMEM((SLOTS // 2, 2 * GROUP, WIDTH), BF16),
            pltpu.VMEM((SLOTS // 2, 2 * GROUP, STATE), BF16),
            pltpu.VMEM((CHUNK, COLS), F32),
            pltpu.VMEM((CHUNK, 2 * COLS), BF16),
            pltpu.VMEM((OWNERS, 32, 128), BF16),
            pltpu.VMEM((256, WIDTH), BF16),
            pltpu.SemaphoreType.DMA((SLOTS + 3,)),
        ],
        out_shape=shape((FRAMES, WIDTH), BF16),
        compiler_params=mid_params,
        name="finish",
    )(near, c_t, far, far_pair, carry)


def solution(mesh):
    return jax.shard_map(
        shards,
        mesh=mesh,
        in_specs=(P("seq", "head"), P("head", "seq"), P("head", "seq"), P("head"), P("seq")),
        out_specs=P("seq", "head"),
        check_vma=False,
    )
```
